32 devices in a mesh: dp: 8 (over y, x, core), tensor: 4 (over z).
Axes of the slice: x: 2, y: 2, z: 4, core: 2. Of those that a mesh axis runs over, the one named last changes fastest.
Arguments:
- wq_flat: bfloat16 [8192, 4096], P(('dp', 'tensor')), may hold values from -0.125 to 0.125
- hidden: bfloat16 [4, 16, 8192], P(None, 'dp'), may hold values from -6 to 6
- cache: bfloat16 [16, 4, 8192, 256], P('dp', None, 'tensor'), may hold values from -300 to 300
- new_kv: bfloat16 [4, 16, 4, 256], P(None, 'dp'), may hold values from -6 to 6
- lengths: int32 [16], P('dp'), may hold values from 1 to 8192, as said below
Outputs:
- attended: bfloat16 [4, 16, 4096], P(None, 'dp', 'tensor')
The draws below stay inside these ranges and needn't reach their ends.
Inputs may be any that keep to these rules, and one draw needn't show every extreme that they name: `lengths`: every sequence has at least one cached position; in every draw some sequence has exactly 8192.
All inputs are finite; a program needn't handle non-finite values.
Results may differ from the reference program's by a relative error of at most 0.03.
Values may be sent and summed in bfloat16 or wider, within the bound.
A program may use at most 64 MiB of HBM per device.

```python
import jax
import jax.numpy as jnp
from jax import lax

D = 8192
QH = 32
KVH = 4
HD = 128
STEPS = 4
CTX = 8192
QW = 4096
SEQS = 16


def draw_cache(key, part):
    base = jnp.clip(jax.random.normal(key, (SEQS, KVH, CTX, 2 * HD), jnp.float32), -6.0, 6.0)
    factor = jnp.full((SEQS, KVH, CTX, 1), 3.0, jnp.float32)
    base = jnp.concatenate([base[..., :HD] * factor, base[..., HD:]], axis=-1)
    return base.astype(jnp.bfloat16)


def draw_lengths(key, part):
    key_len = jax.random.fold_in(key, 21)
    key_pick = jax.random.fold_in(key, 22)
    spans = jax.random.randint(key_len, (SEQS,), 1, CTX + 1)
    chosen = jax.random.randint(key_pick, (), 0, SEQS)
    return jnp.where(jnp.arange(SEQS) == chosen, CTX, spans).astype(jnp.int32)


def raised(values, key, source, target, parts, factor):
    def block_of(dim):
        return (jnp.arange(values.shape[dim]) // (values.shape[dim] // parts)).reshape((-1,) + (1,) * (values.ndim - 1 - dim))

    first = jax.random.permutation(key, parts)[block_of(target)]
    second = (block_of(target) + parts // 2) % parts
    return jnp.where((block_of(source) == first) | (block_of(source) == second), factor * values, values)


def block_scale(rng, dims, shards, low, largest):
    loudness = 1.0
    for axis_at, blocks in shards:
        draws = jax.random.uniform(jax.random.fold_in(jax.random.fold_in(rng, 6), axis_at), (blocks,), jnp.float32, low / len(shards), largest / len(shards))
        loudness = loudness * jnp.repeat(jnp.exp(draws), dims[axis_at] // blocks).reshape((-1,) + (1,) * (len(dims) - 1 - axis_at))
    return loudness


def centred(key, shape, deviation, bound, pieces=(), dtype=jnp.bfloat16):
    array = jax.random.normal(key, shape, jnp.float32) * deviation
    if len(pieces) > 0:
        array = block_scale(key, shape, pieces, -0.22, 0.18) * array
    return jnp.clip(array, min=-bound, max=bound).astype(dtype)


def bell_draw_with(rng, extent, scale, reach, cuts, heavy, dtype=jnp.bfloat16):
    entries = scale * jax.random.normal(rng, extent, jnp.float32)
    if cuts:
        entries = entries * block_scale(rng, extent, cuts, -0.22, 0.18)
    return jnp.clip(raised(entries, jax.random.fold_in(rng, 3), *heavy), -reach, reach).astype(dtype)


def setup_inputs(seed: int = 0) -> dict:
    key_list = jax.random.split(jax.random.key(seed), 6)
    wq_flat = bell_draw_with(key_list[0], (D, QW), D ** -0.5, 0.125, ((0, 32),), (0, 1, 32, 2.75))
    hidden = centred(key_list[1], (STEPS, SEQS, D), 1.0, 6.0, ((1, 8),))
    cache = draw_cache(jax.random.fold_in(key_list[5], 71), 0)
    new_kv = centred(key_list[3], (STEPS, SEQS, KVH, 2 * HD), 1.0, 6.0, ((1, 8),))
    lengths = draw_lengths(jax.random.fold_in(key_list[5], 71), 0)
    return dict(wq_flat=wq_flat, hidden=hidden, cache=cache, new_kv=new_kv, lengths=lengths)


def reference(wq_flat, hidden, cache, new_kv, lengths):
    group = QH // KVH
    scale = 1.0 / (HD ** 0.5)
    rows = STEPS * SEQS
    query = jnp.dot(hidden.reshape(rows, D), wq_flat, preferred_element_type=jnp.float32).astype(jnp.bfloat16)
    query = query.reshape(STEPS, SEQS, KVH, group, HD).transpose(1, 0, 2, 3, 4)
    fresh_all = new_kv.transpose(1, 0, 2, 3)
    causal = jnp.arange(STEPS)[:, None] >= jnp.arange(STEPS)[None, :]

    def one_sequence(items):
        queries, stored, fresh, length = items
        queries = queries.astype(jnp.float32)
        keys = stored[..., :HD].astype(jnp.float32)
        values = stored[..., HD:].astype(jnp.float32)
        new_keys = fresh[..., :HD].astype(jnp.float32)
        new_values = fresh[..., HD:].astype(jnp.float32)
        valid = (jnp.arange(CTX) < length)[None, None, None, :]
        old_scores = jnp.einsum("tgjd,gcd->gtjc", queries, keys) * scale
        old_scores = jnp.where(valid, old_scores, -1e30)
        new_scores = jnp.einsum("tgjd,ugd->gtju", queries, new_keys) * scale
        mask_new = causal[None, :, None, :]
        new_scores = jnp.where(mask_new, new_scores, -1e30)
        top = jnp.maximum(jnp.max(old_scores, axis=-1), jnp.max(new_scores, axis=-1))
        old_w = jnp.where(valid, jnp.exp(old_scores - top[..., None]), 0.0)
        new_w = jnp.where(mask_new, jnp.exp(new_scores - top[..., None]), 0.0)
        total = jnp.sum(old_w, axis=-1) + jnp.sum(new_w, axis=-1)
        old_r = old_w.astype(jnp.bfloat16).astype(jnp.float32)
        new_r = new_w.astype(jnp.bfloat16).astype(jnp.float32)
        accum = jnp.einsum("gtjc,gcd->gtjd", old_r, values) + jnp.einsum("gtju,ugd->gtjd", new_r, new_values)
        out = accum / total[..., None]
        return out.transpose(1, 0, 2, 3).reshape(STEPS, QH * HD).astype(jnp.bfloat16)

    result = lax.map(one_sequence, (query, cache, fresh_all, lengths))
    return result.transpose(1, 0, 2)
```

```python
import functools

import jax
import jax.numpy as jnp
from jax import lax
from jax.experimental import pallas as pl
from jax.experimental.pallas import tpu as pltpu
from jax.sharding import PartitionSpec as P

QH = 32
HD = 128
MESH = pl.DeviceIdType.MESH
NEG = -1e30


def kernel(
    n,
    nt,
    blocked,
    lengths,
    hid_any,
    blocks,
    new_any,
    wq,
    cache,
    out,
    hid,
    new_kv,
    sem_in,
    wq_out,
    wq_all,
    kv,
    fresh,
    x_sc,
    xg,
    yown,
    ysend,
    yrecv,
    zsend,
    qbuf,
    q_sc,
    acc_sc,
    asend,
    arecv,
    m_sc,
    l_sc,
    ssend,
    srecv,
    sem_w,
    sem_kv,
    sx_s,
    sx_r,
    sy_s,
    sy_r,
    sp_s,
    sp_r,
    sq_s,
    sq_r,
    sa_s,
    sa_r,
    ss_s,
    ss_r,
):
    d = lax.axis_index("dp")
    t = lax.axis_index("tensor")
    core = lax.rem(d, 2)
    chip = d // 2
    chips = n // 2
    mate = d + 1 - 2 * core
    steps, seqs, width = hid.shape
    _, depth, half = wq_all.shape
    rows = steps * seqs
    _, kvh, ctx, _ = kv.shape
    drains = []
    heads = QH // nt
    group = QH // kvh
    scale = 1.0 / HD**0.5

    load_hid = pltpu.make_async_copy(hid_any, hid, sem_in.at[0])
    load_new = pltpu.make_async_copy(new_any, new_kv, sem_in.at[1])
    load_hid.start()
    load_new.start()
    load_out = pltpu.make_async_copy(
        wq.at[:, pl.ds(pl.multiple_of((1 - core) * half, half), half)], wq_out, sem_w.at[0]
    )
    load_own = pltpu.make_async_copy(
        wq.at[:, pl.ds(pl.multiple_of(core * half, half), half)], wq_all.at[core], sem_w.at[1]
    )
    load_out.start()
    load_own.start()
    load_kv = [
        [pltpu.make_async_copy(cache.at[s, g], kv.at[s, g], sem_kv.at[s, g]) for g in range(kvh)]
        for s in range(seqs)
    ]
    barrier = pltpu.get_barrier_semaphore()

    @pl.loop(1, n)
    def _(k):
        pl.semaphore_signal(
            barrier, inc=1, device_id=(lax.rem(d + k, n), t), device_id_type=MESH
        )

    @pl.loop(1, nt)
    def _(k):
        peer = lax.rem(t + k, nt)
        pl.semaphore_signal(barrier, inc=1, device_id=(d, peer), device_id_type=MESH)
        pl.semaphore_signal(barrier, inc=1, device_id=(mate, peer), device_id_type=MESH)

    pl.semaphore_wait(barrier, n - 1 + 2 * (nt - 1))

    load_hid.wait()
    load_new.wait()

    def columns_of(block):
        if blocked:
            return blocks.at[block]
        start = pl.multiple_of((block * nt + t) * depth, depth)
        return hid.at[:, :, pl.ds(start, depth)]

    def chip_at(k):
        return lax.rem(chip % 2 + k % 2, 2) + 2 * lax.rem(chip // 2 + k // 2, chips // 2)

    def peer_at(k):
        return 2 * chip_at(k // 2) + lax.rem(core + k % 2, 2)

    def x_copy(k, b, slot, peer, source):
        return pltpu.make_async_remote_copy(
            src_ref=columns_of(2 * (peer // 2) + b),
            dst_ref=xg.at[b, slot],
            send_sem=sx_s.at[k, b],
            recv_sem=sx_r.at[source, b],
            device_id=(peer, t),
            device_id_type=MESH,
        )

    push = pltpu.make_async_remote_copy(
        src_ref=wq_out,
        dst_ref=wq_all.at[core],
        send_sem=sp_s.at[core],
        recv_sem=sp_r.at[core],
        device_id=(mate, t),
        device_id_type=MESH,
    )
    pull = pltpu.make_async_remote_copy(
        src_ref=wq_out,
        dst_ref=wq_all.at[1 - core],
        send_sem=sp_s.at[core],
        recv_sem=sp_r.at[1 - core],
        device_id=(mate, t),
        device_id_type=MESH,
    )

    @pl.loop(1, n)
    def _(k):
        for b in range(2):
            x_copy(n - k, b, d, peer_at(n - k), d).start()

    load_out.wait()
    push.start()
    for b in range(2):
        xg[b, d] = columns_of(2 * chip + b)[...]
    for g in range(kvh):
        for s in range(seqs):
            load_kv[s][g].start()
    for i in range(steps):
        for s in range(seqs):
            r = (i * seqs + s) * kvh
            fresh[r : r + kvh, :] = new_kv[i, s].astype(jnp.float32)
    load_own.wait()
    pull.wait_recv()

    @pl.loop(1, n)
    def _(k):
        peer = peer_at(k)
        for b in range(2):
            x_copy(k, b, peer, peer, peer).wait_recv()

    def x_drain():
        push.wait_send()

        @pl.loop(1, n)
        def _(k):
            for b in range(2):
                x_copy(k, b, d, peer_at(k), d).wait_send()

    drains.append(x_drain)
    xs = []
    for b in range(2):
        if blocked:
            xs.append(xg[b].reshape(n * rows, depth).astype(jnp.bfloat16))
        else:
            for p in range(n):
                for i in range(steps):
                    r = p * rows + i * seqs
                    x_sc[b, r : r + seqs, :] = xg[b, p, i].astype(jnp.float32)
            xs.append(x_sc[b].astype(jnp.bfloat16))

    cuts = ysend.shape[0]
    wide = half // cuts

    def y_copy(c, k, slot, peer, source):
        return pltpu.make_async_remote_copy(
            src_ref=ysend.at[c, peer],
            dst_ref=yrecv.at[c, slot],
            send_sem=sy_s.at[c, k],
            recv_sem=sy_r.at[c, source],
            device_id=(2 * peer + core, t),
            device_id_type=MESH,
        )

    for c in range(cuts):
        y = sum(
            jnp.dot(
                xs[b], wq_all[b, :, c * wide : (c + 1) * wide], preferred_element_type=jnp.float32
            )
            for b in range(2)
        ).reshape(chips, 2 * rows, wide)
        ysend[c] = y.astype(jnp.bfloat16)
        yown[c] = y

        @pl.loop(1, chips)
        def _(k):
            y_copy(c, chips - k, chip, chip_at(chips - k), chip).start()

    mine = core * nt + t

    def q_copy(c, k, which, peer_core, peer, slot):
        return pltpu.make_async_remote_copy(
            src_ref=zsend.at[c, peer_core],
            dst_ref=qbuf.at[c, slot],
            send_sem=sq_s.at[c, k, which],
            recv_sem=sq_r.at[c, slot],
            device_id=(2 * chip + peer_core, peer),
            device_id_type=MESH,
        )

    for c in range(cuts):

        def y_add(k, z):
            p = chip_at(k)
            y_copy(c, k, p, p, p).wait_recv()
            return z + yrecv[c, p].astype(jnp.float32)

        z = lax.fori_loop(1, chips, y_add, yown[c, chip])
        for i in range(2):
            zsend[c, i] = z[i * rows : (i + 1) * rows].astype(zsend.dtype)

        @pl.loop(1, nt)
        def _(k):
            peer = lax.rem(t + k, nt)
            q_copy(c, k, 0, core, peer, mine).start()
            q_copy(c, k, 1, 1 - core, peer, mine).start()

        q_copy(c, 0, 1, 1 - core, t, mine).start()
        qbuf[c, mine] = zsend[c, core]

    def q_drain():
        for c in range(cuts):
            pl.loop(1, chips)(lambda k: y_copy(c, k, chip, chip_at(k), chip).wait_send())
            q_copy(c, 0, 1, 1 - core, t, mine).wait_send()

            @pl.loop(1, nt)
            def _(k):
                peer = lax.rem(t + k, nt)
                q_copy(c, k, 0, core, peer, mine).wait_send()
                q_copy(c, k, 1, 1 - core, peer, mine).wait_send()

    drains.append(q_drain)

    band = group * rows
    position = t * ctx + lax.broadcasted_iota(jnp.int32, (1, ctx), 1)
    owned = heads * rows
    eye = lax.broadcasted_iota(jnp.int32, (owned, HD), 0) == lax.broadcasted_iota(
        jnp.int32, (owned, HD), 1
    )

    def a_copy(slot, peer, source):
        return pltpu.make_async_remote_copy(
            src_ref=asend.at[peer],
            dst_ref=arecv.at[slot],
            send_sem=sa_s.at[peer],
            recv_sem=sa_r.at[source],
            device_id=(d, peer),
            device_id_type=MESH,
        )

    def s_copy(slot, peer, source):
        return pltpu.make_async_remote_copy(
            src_ref=ssend.at[peer],
            dst_ref=srecv.at[slot],
            send_sem=ss_s.at[peer],
            recv_sem=ss_r.at[source],
            device_id=(d, peer),
            device_id_type=MESH,
        )

    def attend(g, s):
        base = pl.ds(pl.multiple_of(g * band, band), band)
        span = pl.ds(s, group * steps, stride=seqs)
        q = q_sc.at[base][span, :].astype(jnp.bfloat16)
        scores = lax.dot_general(
            q, kv[s, g, :, :HD], (((1,), (1,)), ((), ())), preferred_element_type=jnp.float32
        )
        masked = jnp.where(position < lengths[s], scores * scale, NEG)
        best = jnp.max(masked, axis=-1, keepdims=True)
        weights = jnp.exp(masked - best)
        total = jnp.sum(weights, axis=-1, keepdims=True)
        acc = jnp.dot(
            weights.astype(jnp.bfloat16), kv[s, g, :, HD:], preferred_element_type=jnp.float32
        )
        acc_sc.at[base][span, :] = acc
        m_sc.at[base][span, :] = jnp.broadcast_to(best, acc.shape)
        l_sc.at[base][span, :] = jnp.broadcast_to(total, acc.shape)

    side = kvh // 2 // cuts
    per = group // heads
    far = (2 * t < nt).astype(jnp.int32)
    for c in range(cuts):
        q_copy(c, 0, 1, 1 - core, t, (1 - core) * nt + t).wait_recv()

        @pl.loop(1, nt)
        def _(k):
            peer = lax.rem(t + k, nt)
            q_copy(c, k, 0, core, peer, core * nt + peer).wait_recv()
            q_copy(c, k, 1, core, peer, (1 - core) * nt + peer).wait_recv()

        for i in range(2):
            total = qbuf[c, i * nt].astype(jnp.float32)
            for j in range(1, nt):
                total = total + qbuf[c, i * nt + j].astype(jnp.float32)
            first = (i * half + c * wide) // HD
            for j in range(wide // HD):
                h = first + j
                q_sc[h * rows : (h + 1) * rows, :] = total[:, j * HD : (j + 1) * HD]

        ready = [i * (kvh // 2) + c * side + j for i in range(2) for j in range(side)]
        for g in ready:
            for s in range(seqs):
                load_kv[s][g].wait()
        for low, high in zip(ready, ready[::-1]):
            g = low + (high - low) * far
            for s in range(seqs):
                attend(g, s)
            for i in range(per):
                j = g * per + i
                window = pl.ds(pl.multiple_of(j * owned, owned), owned)
                asend[j] = acc_sc[window, :].astype(asend.dtype)
                for at, ref in enumerate((m_sc, l_sc)):
                    ssend[j, at : at + 1, :] = jnp.sum(
                        jnp.where(eye, ref[window, :], 0.0), axis=0, keepdims=True
                    )

                @pl.when(t != j)
                def _():
                    a_copy(t, j, t).start()
                    s_copy(t, j, t).start()

    own = pl.ds(pl.multiple_of(t * owned, owned), owned)
    q_own = q_sc[own, :].astype(jnp.bfloat16)
    new_keys = fresh[:, :HD].astype(jnp.bfloat16)
    new_values = fresh[:, HD:].astype(jnp.bfloat16)
    new_scores = (
        lax.dot_general(
            q_own, new_keys, (((1,), (1,)), ((), ())), preferred_element_type=jnp.float32
        )
        * scale
    )
    row = lax.broadcasted_iota(jnp.int32, new_scores.shape, 0)
    col = lax.broadcasted_iota(jnp.int32, new_scores.shape, 1)
    col_row = col // kvh
    causal = (
        (lax.rem(col, kvh) == t * heads // group)
        & (lax.rem(row, seqs) == lax.rem(col_row, seqs))
        & (lax.rem(row, rows) // seqs >= col_row // seqs)
    )
    new_masked = jnp.where(causal, new_scores, NEG)
    top = jnp.max(new_masked, axis=-1, keepdims=True)
    new_weights = jnp.where(causal, jnp.exp(new_masked - top), 0.0)
    denom = jnp.sum(new_weights, axis=-1, keepdims=True)
    accum = jnp.dot(
        new_weights.astype(jnp.bfloat16), new_values, preferred_element_type=jnp.float32
    )

    def join(state, best, total, acc):
        top, denom, accum = state
        peak = jnp.maximum(top, best)
        left = jnp.exp(top - peak)
        right = jnp.exp(best - peak)
        return peak, denom * left + total * right, accum * left + acc * right

    state = join((top, denom, accum), m_sc[own, :][:, :1], l_sc[own, :][:, :1], acc_sc[own, :])

    def a_join(k, state):
        peer = lax.rem(t + k, nt)
        a_copy(peer, peer, peer).wait_recv()
        s_copy(peer, peer, peer).wait_recv()
        stats = srecv[peer]
        best = jnp.sum(jnp.where(eye, stats[0:1, :], 0.0), axis=1, keepdims=True)
        total = jnp.sum(jnp.where(eye, stats[1:2, :], 0.0), axis=1, keepdims=True)
        return join(state, best, total, arecv[peer].astype(jnp.float32))

    top, denom, accum = lax.fori_loop(1, nt, a_join, state)
    result = accum / denom
    for j in range(heads):
        for i in range(steps):
            r = j * rows + i * seqs
            out[i, :, j * HD : (j + 1) * HD] = result[r : r + seqs].astype(out.dtype)

    def a_drain():
        @pl.loop(1, nt)
        def _(k):
            peer = lax.rem(t + k, nt)
            a_copy(t, peer, t).wait_send()
            s_copy(t, peer, t).wait_send()

    drains.append(a_drain)
    for drain in drains:
        drain()


def body(wq_flat, hidden, cache, new_kv, lengths):
    nt = lax.axis_size("tensor")
    n = lax.axis_size("dp")
    t = lax.axis_index("tensor")
    steps, seqs, width = hidden.shape
    rows = steps * seqs
    depth, columns = wq_flat.shape
    kvh, ctx = cache.shape[1], cache.shape[2]
    half = columns // 2
    cuts = 2 if kvh % 4 == 0 else 1
    wide = half // cuts
    heads = QH // nt
    owned = heads * rows
    chips = n // 2
    bf16, f32 = jnp.bfloat16, jnp.float32
    dma = pltpu.SemaphoreType.DMA
    vmem = pl.BlockSpec(memory_space=pltpu.VMEM)
    blocked = depth % 128 != 0
    blocks = hidden
    if blocked:
        blocks = hidden.reshape(rows, n, nt, depth)
        blocks = lax.dynamic_index_in_dim(blocks, t, 2, keepdims=False).astype(f32)
        blocks = blocks.transpose(1, 0, 2)
    held = (rows, depth) if blocked else (steps, seqs, depth)
    anywhere = pl.BlockSpec(memory_space=pl.ANY)
    result = pl.pallas_call(
        functools.partial(kernel, n, nt, blocked),
        out_shape=pltpu.VMEM((steps, seqs, heads * HD), f32),
        in_specs=[pl.BlockSpec(memory_space=pltpu.SMEM), anywhere, vmem if blocked else anywhere, anywhere, anywhere, anywhere],
        out_specs=vmem,
        scratch_shapes=[
            pltpu.VMEM(hidden.shape, bf16),
            pltpu.VMEM(new_kv.shape, bf16),
            dma((2,)),
            pltpu.VMEM((depth, half), bf16),
            pltpu.VMEM((2, depth, half), bf16),
            pltpu.VMEM(cache.shape, bf16),
            pltpu.VMEM((rows * kvh, 2 * HD), f32),
            pltpu.VMEM((2, n * rows, depth), f32),
            pltpu.VMEM((2, n, *held), blocks.dtype),
            pltpu.VMEM((cuts, chips, 2 * rows, wide), f32),
            pltpu.VMEM((cuts, chips, 2 * rows, wide), bf16),
            pltpu.VMEM((cuts, chips, 2 * rows, wide), bf16),
            pltpu.VMEM((cuts, 2, rows, wide), bf16),
            pltpu.VMEM((cuts, 2 * nt, rows, wide), bf16),
            pltpu.VMEM((QH * rows, HD), f32),
            pltpu.VMEM((QH * rows, HD), f32),
            pltpu.VMEM((nt, owned, HD), bf16),
            pltpu.VMEM((nt, owned, HD), bf16),
            pltpu.VMEM((QH * rows, HD), f32),
            pltpu.VMEM((QH * rows, HD), f32),
            pltpu.VMEM((nt, 8, HD), f32),
            pltpu.VMEM((nt, 8, HD), f32),
            dma((2,)),
            dma((seqs, kvh)),
            dma((n, 2)),
            dma((n, 2)),
            dma((cuts, chips)),
            dma((cuts, chips)),
            dma((2,)),
            dma((2,)),
            dma((cuts, nt, 2)),
            dma((cuts, 2 * nt)),
            dma((nt,)),
            dma((nt,)),
            dma((nt,)),
            dma((nt,)),
        ],
        compiler_params=pltpu.CompilerParams(collective_id=0, has_side_effects=True),
    )(lengths, hidden, blocks, new_kv, wq_flat, cache)
    return result.astype(bf16)


def solution(mesh):
    placed = (
        P(("dp", "tensor"), None),
        P(None, "dp", None),
        P("dp", None, "tensor", None),
        P(None, "dp", None, None),
        P("dp"),
    )
    return jax.shard_map(
        body, mesh=mesh, in_specs=placed, out_specs=P(None, "dp", "tensor"), check_vma=False
    )
```

```python
import functools

import jax
import jax.numpy as jnp
from jax import lax
from jax.experimental import pallas as pl
from jax.experimental.pallas import tpu as pltpu
from jax.sharding import PartitionSpec as P

QH = 32
HD = 128
MESH = pl.DeviceIdType.MESH
NEG = -1e30


def kernel(
    n,
    nt,
    blocked,
    lengths_any,
    hid_any,
    blocks,
    new_any,
    wq,
    cache,
    out,
    hid,
    new_kv,
    lengths,
    sem_in,
    wq_out,
    wq_all,
    kv,
    fresh,
    x_sc,
    xg,
    yown,
    ysend,
    yrecv,
    zsend,
    qbuf,
    q_sc,
    r_sc,
    asend,
    arecv,
    ssend,
    srecv,
    sem_w,
    sem_kv,
    sx_s,
    sx_r,
    sy_s,
    sy_r,
    sp_s,
    sp_r,
    sq_s,
    sq_r,
    sa_s,
    sa_r,
    ss_s,
    ss_r,
):
    d = lax.axis_index("dp")
    t = lax.axis_index("tensor")
    core = lax.rem(d, 2)
    chip = d // 2
    chips = n // 2
    mate = d + 1 - 2 * core
    steps, seqs, width = hid.shape
    _, depth, half = wq_all.shape
    rows = steps * seqs
    _, kvh, ctx, _ = kv.shape
    drains = []
    heads = QH // nt
    group = QH // kvh
    scale = 1.0 / HD**0.5

    load_hid = pltpu.make_async_copy(hid_any, hid, sem_in.at[0])
    load_new = pltpu.make_async_copy(new_any, new_kv, sem_in.at[1])
    load_lengths = pltpu.make_async_copy(lengths_any, lengths, sem_in.at[2])
    load_hid.start()
    load_lengths.start()
    load_new.start()
    load_out = pltpu.make_async_copy(
        wq.at[:, pl.ds(pl.multiple_of((1 - core) * half, half), half)], wq_out, sem_w.at[0]
    )
    load_own = pltpu.make_async_copy(
        wq.at[:, pl.ds(pl.multiple_of(core * half, half), half)], wq_all.at[core], sem_w.at[1]
    )
    load_out.start()
    load_own.start()
    load_kv = [
        [pltpu.make_async_copy(cache.at[s, g], kv.at[s, g], sem_kv) for g in range(kvh)]
        for s in range(seqs)
    ]
    barrier = pltpu.get_barrier_semaphore()

    @pl.loop(1, n)
    def _(k):
        pl.semaphore_signal(
            barrier, inc=1, device_id=(lax.rem(d + k, n), t), device_id_type=MESH
        )

    @pl.loop(1, nt)
    def _(k):
        peer = lax.rem(t + k, nt)
        pl.semaphore_signal(barrier, inc=1, device_id=(d, peer), device_id_type=MESH)
        pl.semaphore_signal(barrier, inc=1, device_id=(mate, peer), device_id_type=MESH)

    pl.semaphore_wait(barrier, n - 1 + 2 * (nt - 1))

    load_hid.wait()
    load_new.wait()
    load_lengths.wait()

    def columns_of(block):
        if blocked:
            return blocks.at[block]
        start = pl.multiple_of((block * nt + t) * depth, depth)
        return hid.at[:, :, pl.ds(start, depth)]

    def whole(ref, send_sem, recv_sem):
        return pltpu.make_async_remote_copy(
            src_ref=ref,
            dst_ref=ref,
            send_sem=send_sem,
            recv_sem=recv_sem,
            device_id=(mate, t),
            device_id_type=MESH,
        )

    def chip_at(k):
        return lax.rem(chip % 2 + k % 2, 2) + 2 * lax.rem(chip // 2 + k // 2, chips // 2)

    def peer_at(k):
        return 2 * chip_at(k // 2) + lax.rem(core + k % 2, 2)

    def x_copy(b, peer):
        return pltpu.make_async_remote_copy(
            src_ref=columns_of(2 * (peer // 2) + b),
            dst_ref=xg.at[b, d],
            send_sem=sx_s,
            recv_sem=sx_r,
            device_id=(peer, t),
            device_id_type=MESH,
        )

    push = pltpu.make_async_remote_copy(
        src_ref=wq_out,
        dst_ref=wq_all.at[core],
        send_sem=sp_s,
        recv_sem=sp_r,
        device_id=(mate, t),
        device_id_type=MESH,
    )
    @pl.loop(1, n)
    def _(k):
        for b in range(2):
            x_copy(b, peer_at(n - k)).start()

    load_out.wait()
    push.start()
    for b in range(2):
        xg[b, d] = columns_of(2 * chip + b)[...]
    for g in range(kvh):
        for s in range(seqs):
            load_kv[s][g].start()
    for i in range(steps):
        for s in range(seqs):
            r = (i * seqs + s) * kvh
            fresh[r : r + kvh, :] = new_kv[i, s].astype(jnp.float32)
    load_own.wait()
    push.wait_recv()

    x_all = whole(xg.at[:, pl.ds(0, n - 1)], sx_s, sx_r)
    x_all.wait_recv()
    drains.append(push.wait_send)
    drains.append(x_all.wait_send)
    _, tiles, _, lanes = x_sc.shape
    xs = []
    for b in range(2):
        for p in range(n):
            if blocked:
                for s in range(seqs):
                    r = (s * n + p) * steps
                    x_sc[b, 0, r : r + steps, :] = xg[b, p, s * steps : (s + 1) * steps]
            else:
                for i in range(steps):
                    lines = pl.ds(p * steps + i, seqs, stride=n * steps)
                    block = xg[b, p, i].astype(jnp.float32)
                    for h in range(tiles):
                        x_sc.at[b, h][lines, :] = block[:, h * lanes : (h + 1) * lanes]
        xs.append(jnp.concatenate([x_sc[b, h] for h in range(tiles)], axis=1).astype(jnp.bfloat16))

    cuts = ysend.shape[0]
    wide = half // cuts

    def y_copy(c, s, peer):
        return pltpu.make_async_remote_copy(
            src_ref=ysend.at[c, s, peer],
            dst_ref=yrecv.at[c, s, chip],
            send_sem=sy_s,
            recv_sem=sy_r.at[c, s],
            device_id=(2 * peer + core, t),
            device_id_type=MESH,
        )

    for c in range(cuts):
        at = c + core * (cuts - 1 - 2 * c)
        columns = pl.ds(pl.multiple_of(at * wide, wide), wide)
        y = sum(
            jnp.dot(xs[b], wq_all[b, :, columns], preferred_element_type=jnp.float32)
            for b in range(2)
        ).reshape(seqs, chips, 2 * steps, wide)
        for s in range(seqs):
            ysend[c, s] = y[s].astype(jnp.bfloat16)
            yown[c, s] = y[s]

            @pl.loop(1, chips)
            def _(k):
                y_copy(c, s, chip_at(chips - k)).start()

    mine = core * nt + t

    def q_copy(c, s, peer_core, peer):
        return pltpu.make_async_remote_copy(
            src_ref=zsend.at[c, s, peer_core],
            dst_ref=qbuf.at[c, s, mine],
            send_sem=sq_s,
            recv_sem=sq_r.at[c, s],
            device_id=(2 * chip + peer_core, peer),
            device_id_type=MESH,
        )

    for c in range(cuts):
        for s in range(seqs):
            whole(yrecv.at[c, s, pl.ds(0, chips - 1)], sy_s, sy_r.at[c, s]).wait_recv()
            z = yown[c, s, chip]
            for k in range(1, chips):
                z = z + yrecv[c, s, chip_at(k)].astype(jnp.float32)
            for i in range(2):
                zsend[c, s, i] = z[i * steps : (i + 1) * steps].astype(zsend.dtype)

            @pl.loop(1, nt)
            def _(k):
                peer = lax.rem(t + nt - k, nt)
                q_copy(c, s, core, peer).start()
                q_copy(c, s, 1 - core, peer).start()

            q_copy(c, s, 1 - core, t).start()
            qbuf[c, s, mine] = zsend[c, s, core]

    drains.append(whole(ysend.at[:, :, pl.ds(0, chips - 1)], sy_s, sy_r.at[0, 0]).wait_send)
    drains.append(whole(qbuf.at[:, :, pl.ds(0, 2 * nt - 1)], sq_s, sq_r.at[0, 0]).wait_send)

    band = group * steps
    owned = heads * steps
    position = t * ctx + lax.broadcasted_iota(jnp.int32, (1, ctx), 1)
    eye = lax.broadcasted_iota(jnp.int32, (owned, HD), 0) == lax.broadcasted_iota(
        jnp.int32, (owned, HD), 1
    )

    def a_copy(peer, s):
        return pltpu.make_async_remote_copy(
            src_ref=asend.at[s, peer],
            dst_ref=arecv.at[s, t],
            send_sem=sa_s,
            recv_sem=sa_r,
            device_id=(d, peer),
            device_id_type=MESH,
        )

    def s_copy(peer, s):
        return pltpu.make_async_remote_copy(
            src_ref=ssend.at[s, peer],
            dst_ref=srecv.at[s, t],
            send_sem=ss_s,
            recv_sem=ss_r,
            device_id=(d, peer),
            device_id_type=MESH,
        )

    def attend(g, s):
        base = pl.multiple_of((g * seqs + s) * band, band)
        q = q_sc[pl.ds(base, band), :].astype(jnp.bfloat16)
        scores = lax.dot_general(
            q, kv[s, g, :, :HD], (((1,), (1,)), ((), ())), preferred_element_type=jnp.float32
        )
        masked = jnp.where(position < lengths[s], scores * scale, NEG)
        best = jnp.max(masked, axis=-1, keepdims=True)
        weights = jnp.exp(masked - best)
        total = jnp.sum(weights, axis=-1, keepdims=True)
        acc = jnp.dot(
            weights.astype(jnp.bfloat16), kv[s, g, :, HD:], preferred_element_type=jnp.float32
        )
        for i in range(per):
            lines = slice(i * owned, (i + 1) * owned)
            asend[s, g * per + i] = acc[lines].astype(asend.dtype)
            for at, stat in enumerate((best, total)):
                ssend[s, g * per + i, at : at + 1, :] = jnp.sum(
                    jnp.where(eye, stat[lines], 0.0), axis=0, keepdims=True
                )

    side = kvh // 2 // cuts
    per = group // heads
    far = (2 * t < nt).astype(jnp.int32)
    pltpu.make_async_copy(cache, kv, sem_kv).wait()
    for c in range(cuts):
        sides = (c, 2 * cuts - 1 - c)
        ready = [i * side + j for i in sides for j in range(side)]
        for s in range(seqs):
            whole(qbuf.at[c, s, pl.ds(0, 2 * nt - 1)], sq_s, sq_r.at[c, s]).wait_recv()
            for i in range(2):
                total = qbuf[c, s, i * nt].astype(jnp.float32)
                for j in range(1, nt):
                    total = total + qbuf[c, s, i * nt + j].astype(jnp.float32)
                for j in range(wide // HD):
                    g = sides[i] * side + j // group
                    r = ((g * seqs + s) * group + j % group) * steps
                    q_sc[r : r + steps, :] = total[:, j * HD : (j + 1) * HD]
            for low, high in zip(ready, ready[::-1]):
                attend(low + (high - low) * far, s)
            for low, high in zip(ready, ready[::-1]):
                for i in range(per):
                    j = (low + (high - low) * far) * per + i

                    @pl.when(t != j)
                    def _():
                        a_copy(j, s).start()
                        s_copy(j, s).start()

    def mine_at(s):
        r = (t * heads // group * seqs + s) * band + lax.rem(t * heads, group) * steps
        return pl.ds(pl.multiple_of(r, owned), owned)

    q_own = jnp.concatenate([q_sc[mine_at(s), :] for s in range(seqs)]).astype(jnp.bfloat16)
    new_keys = fresh[:, :HD].astype(jnp.bfloat16)
    new_values = fresh[:, HD:].astype(jnp.bfloat16)
    new_scores = (
        lax.dot_general(
            q_own, new_keys, (((1,), (1,)), ((), ())), preferred_element_type=jnp.float32
        )
        * scale
    )
    row = lax.broadcasted_iota(jnp.int32, new_scores.shape, 0)
    col = lax.broadcasted_iota(jnp.int32, new_scores.shape, 1)
    col_row = col // kvh
    causal = (
        (lax.rem(col, kvh) == t * heads // group)
        & (row // owned == lax.rem(col_row, seqs))
        & (lax.rem(row, steps) >= col_row // seqs)
    )
    new_masked = jnp.where(causal, new_scores, NEG)
    top = jnp.max(new_masked, axis=-1, keepdims=True)
    new_weights = jnp.where(causal, jnp.exp(new_masked - top), 0.0)
    denom = jnp.sum(new_weights, axis=-1, keepdims=True)
    accum = jnp.dot(
        new_weights.astype(jnp.bfloat16), new_values, preferred_element_type=jnp.float32
    )

    def join(state, best, total, acc):
        top, denom, accum = state
        peak = jnp.maximum(top, best)
        left = jnp.exp(top - peak)
        right = jnp.exp(best - peak)
        return peak, denom * left + total * right, accum * left + acc * right

    def gathered(parts, stats):
        best, total = (
            jnp.concatenate(
                [
                    jnp.sum(jnp.where(eye, x[at : at + 1, :], 0.0), axis=1, keepdims=True)
                    for x in stats
                ]
            )
            for at in range(2)
        )
        return best, total, jnp.concatenate([x.astype(jnp.float32) for x in parts])

    state = join(
        (top, denom, accum),
        *gathered([asend[s, t] for s in range(seqs)], [ssend[s, t] for s in range(seqs)]),
    )
    a_all = whole(arecv.at[:, pl.ds(0, nt - 1)], sa_s, sa_r)
    s_all = whole(srecv.at[:, pl.ds(0, nt - 1)], ss_s, ss_r)
    a_all.wait_recv()
    s_all.wait_recv()

    def a_join(k, state):
        peer = lax.rem(t + k, nt)
        return join(
            state,
            *gathered([arecv[s, peer] for s in range(seqs)], [srecv[s, peer] for s in range(seqs)]),
        )

    top, denom, accum = lax.fori_loop(1, nt, a_join, state)
    r_sc[...] = accum / denom
    for j in range(heads):
        for i in range(steps):
            lines = pl.ds(j * steps + i, seqs, stride=owned)
            out[i, :, j * HD : (j + 1) * HD] = r_sc[lines, :].astype(out.dtype)

    drains.append(a_all.wait_send)
    drains.append(s_all.wait_send)
    for drain in drains:
        drain()


def body(wq_flat, hidden, cache, new_kv, lengths):
    nt = lax.axis_size("tensor")
    n = lax.axis_size("dp")
    t = lax.axis_index("tensor")
    steps, seqs, width = hidden.shape
    rows = steps * seqs
    depth, columns = wq_flat.shape
    kvh, ctx = cache.shape[1], cache.shape[2]
    half = columns // 2
    cuts = 2 if kvh % 4 == 0 else 1
    wide = half // cuts
    heads = QH // nt
    owned = heads * steps
    chips = n // 2
    bf16, f32 = jnp.bfloat16, jnp.float32
    dma = pltpu.SemaphoreType.DMA
    vmem = pl.BlockSpec(memory_space=pltpu.VMEM)
    blocked = depth % 128 != 0
    blocks = hidden
    if blocked:
        blocks = hidden.transpose(1, 0, 2).reshape(rows, n, nt, depth)
        blocks = lax.dynamic_index_in_dim(blocks, t, 2, keepdims=False).astype(f32)
        blocks = blocks.transpose(1, 0, 2)
    tiles = 1 if blocked else depth // HD
    held = (rows, depth) if blocked else (steps, seqs, depth)
    anywhere = pl.BlockSpec(memory_space=pl.ANY)
    result = pl.pallas_call(
        functools.partial(kernel, n, nt, blocked),
        out_shape=pltpu.VMEM((steps, seqs, heads * HD), f32),
        in_specs=[anywhere, anywhere, vmem if blocked else anywhere, anywhere, anywhere, anywhere],
        out_specs=vmem,
        scratch_shapes=[
            pltpu.VMEM(hidden.shape, bf16),
            pltpu.VMEM(new_kv.shape, bf16),
            pltpu.SMEM(lengths.shape, jnp.int32),
            dma((3,)),
            pltpu.VMEM((depth, half), bf16),
            pltpu.VMEM((2, depth, half), bf16),
            pltpu.VMEM(cache.shape, bf16),
            pltpu.VMEM((rows * kvh, 2 * HD), f32),
            pltpu.VMEM((2, tiles, n * rows, depth // tiles), f32),
            pltpu.VMEM((2, n, *held), blocks.dtype),
            pltpu.VMEM((cuts, seqs, chips, 2 * steps, wide), f32),
            pltpu.VMEM((cuts, seqs, chips, 2 * steps, wide), bf16),
            pltpu.VMEM((cuts, seqs, chips, 2 * steps, wide), bf16),
            pltpu.VMEM((cuts, seqs, 2, steps, wide), bf16),
            pltpu.VMEM((cuts, seqs, 2 * nt, steps, wide), bf16),
            pltpu.VMEM((QH * rows, HD), f32),
            pltpu.VMEM((heads * rows, HD), f32),
            pltpu.VMEM((seqs, nt, owned, HD), bf16),
            pltpu.VMEM((seqs, nt, owned, HD), bf16),
            pltpu.VMEM((seqs, nt, 8, HD), f32),
            pltpu.VMEM((seqs, nt, 8, HD), f32),
            dma((2,)),
            dma(()),
            dma(()),
            dma(()),
            dma(()),
            dma((cuts, seqs)),
            dma(()),
            dma(()),
            dma(()),
            dma((cuts, seqs)),
            dma(()),
            dma(()),
            dma(()),
            dma(()),
        ],
        compiler_params=pltpu.CompilerParams(collective_id=0, has_side_effects=True),
    )(lengths, hidden, blocks, new_kv, wq_flat, cache)
    return result.astype(bf16)


def solution(mesh):
    placed = (
        P(("dp", "tensor"), None),
        P(None, "dp", None),
        P("dp", None, "tensor", None),
        P(None, "dp", None, None),
        P("dp"),
    )
    return jax.shard_map(
        body, mesh=mesh, in_specs=placed, out_specs=P(None, "dp", "tensor"), check_vma=False
    )
```

```python
import functools

import jax
import jax.numpy as jnp
from jax import lax
from jax.experimental import pallas as pl
from jax.experimental.pallas import tpu as pltpu
from jax.sharding import PartitionSpec as P

QH = 32
HD = 128
MESH = pl.DeviceIdType.MESH
NEG = -1e30


def kernel(
    n,
    nt,
    blocked,
    lengths_any,
    hid_any,
    blocks,
    new_any,
    wq,
    cache,
    out,
    hid,
    new_kv,
    lengths,
    sem_in,
    wq_out,
    wq_all,
    kv,
    fresh,
    x_sc,
    xg,
    yown,
    ysend,
    yrecv,
    zsend,
    qbuf,
    q_sc,
    r_sc,
    asend,
    arecv,
    ssend,
    srecv,
    sem_w,
    sem_kv,
    sx_s,
    sx_r,
    sy_s,
    sy_r,
    sp_s,
    sp_r,
    sq_s,
    sq_r,
    sa_s,
    sa_r,
    ss_s,
    ss_r,
):
    d = lax.axis_index("dp")
    t = lax.axis_index("tensor")
    core = lax.rem(d, 2)
    chip = d // 2
    chips = n // 2
    mate = d + 1 - 2 * core
    steps, seqs, width = hid.shape
    _, depth, half = wq_all.shape
    rows = steps * seqs
    _, kvh, ctx, _ = kv.shape
    drains = []
    heads = QH // nt
    group = QH // kvh
    scale = 1.0 / HD**0.5

    load_hid = pltpu.make_async_copy(hid_any, hid, sem_in.at[0])
    load_new = pltpu.make_async_copy(new_any, new_kv, sem_in.at[1])
    load_lengths = pltpu.make_async_copy(lengths_any, lengths, sem_in.at[2])
    load_hid.start()
    load_lengths.start()
    load_new.start()
    load_out = pltpu.make_async_copy(
        wq.at[:, pl.ds(pl.multiple_of((1 - core) * half, half), half)], wq_out, sem_w.at[0]
    )
    load_own = pltpu.make_async_copy(
        wq.at[:, pl.ds(pl.multiple_of(core * half, half), half)], wq_all.at[core], sem_w.at[1]
    )
    load_out.start()
    load_own.start()
    load_kv = [
        [pltpu.make_async_copy(cache.at[s, g], kv.at[s, g], sem_kv) for g in range(kvh)]
        for s in range(seqs)
    ]
    barrier = pltpu.get_barrier_semaphore()

    @pl.loop(1, n)
    def _(k):
        pl.semaphore_signal(
            barrier, inc=1, device_id=(lax.rem(d + k, n), t), device_id_type=MESH
        )

    @pl.loop(1, nt)
    def _(k):
        peer = lax.rem(t + k, nt)
        pl.semaphore_signal(barrier, inc=1, device_id=(d, peer), device_id_type=MESH)
        pl.semaphore_signal(barrier, inc=1, device_id=(mate, peer), device_id_type=MESH)

    pl.semaphore_wait(barrier, n - 1 + 2 * (nt - 1))

    load_hid.wait()
    load_new.wait()
    load_lengths.wait()

    def columns_of(block):
        if blocked:
            return blocks.at[block]
        start = pl.multiple_of((block * nt + t) * depth, depth)
        return hid.at[:, :, pl.ds(start, depth)]

    def whole(ref, send_sem, recv_sem):
        return pltpu.make_async_remote_copy(
            src_ref=ref,
            dst_ref=ref,
            send_sem=send_sem,
            recv_sem=recv_sem,
            device_id=(mate, t),
            device_id_type=MESH,
        )

    def chip_at(k):
        return lax.rem(chip % 2 + k % 2, 2) + 2 * lax.rem(chip // 2 + k // 2, chips // 2)

    def peer_at(k):
        return 2 * chip_at(k // 2) + lax.rem(core + k % 2, 2)

    def x_copy(b, peer):
        return pltpu.make_async_remote_copy(
            src_ref=columns_of(2 * (peer // 2) + b),
            dst_ref=xg.at[b, d],
            send_sem=sx_s,
            recv_sem=sx_r,
            device_id=(peer, t),
            device_id_type=MESH,
        )

    push = pltpu.make_async_remote_copy(
        src_ref=wq_out,
        dst_ref=wq_all.at[core],
        send_sem=sp_s,
        recv_sem=sp_r,
        device_id=(mate, t),
        device_id_type=MESH,
    )
    @pl.loop(1, n)
    def _(k):
        for b in range(2):
            x_copy(b, peer_at(n - k)).start()

    load_out.wait()
    push.start()
    for b in range(2):
        xg[b, d] = columns_of(2 * chip + b)[...]
    for i in range(steps):
        for s in range(seqs):
            r = (i * seqs + s) * kvh
            fresh[r : r + kvh, :] = new_kv[i, s].astype(jnp.float32)
    load_own.wait()
    push.wait_recv()

    x_all = whole(xg.at[:, pl.ds(0, n - 1)], sx_s, sx_r)
    x_all.wait_recv()
    drains.append(push.wait_send)
    drains.append(x_all.wait_send)
    _, tiles, _, lanes = x_sc.shape
    xs = []
    for b in range(2):
        for p in range(n):
            if blocked:
                for s in range(seqs):
                    r = (s * n + p) * steps
                    x_sc[b, 0, r : r + steps, :] = xg[b, p, s * steps : (s + 1) * steps]
            else:
                for i in range(steps):
                    lines = pl.ds(p * steps + i, seqs, stride=n * steps)
                    block = xg[b, p, i].astype(jnp.float32)
                    for h in range(tiles):
                        x_sc.at[b, h][lines, :] = block[:, h * lanes : (h + 1) * lanes]
        xs.append(jnp.concatenate([x_sc[b, h] for h in range(tiles)], axis=1).astype(jnp.bfloat16))

    cuts = ysend.shape[0]
    wide = half // cuts

    def y_copy(c, s, peer):
        return pltpu.make_async_remote_copy(
            src_ref=ysend.at[c, s, peer],
            dst_ref=yrecv.at[c, s, chip],
            send_sem=sy_s,
            recv_sem=sy_r.at[c, s],
            device_id=(2 * peer + core, t),
            device_id_type=MESH,
        )

    for c in range(cuts):
        at = c + core * (cuts - 1 - 2 * c)
        columns = pl.ds(pl.multiple_of(at * wide, wide), wide)
        y = sum(
            jnp.dot(xs[b], wq_all[b, :, columns], preferred_element_type=jnp.float32)
            for b in range(2)
        ).reshape(seqs, chips, 2 * steps, wide)
        for s in range(seqs):
            ysend[c, s] = y[s].astype(jnp.bfloat16)
            yown[c, s] = y[s]

            @pl.loop(1, chips)
            def _(k):
                y_copy(c, s, chip_at(chips - k)).start()

    for g in range(kvh):
        for s in range(seqs):
            load_kv[s][g].start()
    mine = core * nt + t
    far = (2 * t < nt).astype(jnp.int32)

    def q_copy(c, s, peer_core, peer):
        return pltpu.make_async_remote_copy(
            src_ref=zsend.at[c, s, peer_core],
            dst_ref=qbuf.at[c, s, mine],
            send_sem=sq_s,
            recv_sem=sq_r.at[c, s],
            device_id=(2 * chip + peer_core, peer),
            device_id_type=MESH,
        )

    for c in range(cuts):
        for s in range(seqs):
            whole(yrecv.at[c, s, pl.ds(0, chips - 1)], sy_s, sy_r.at[c, s]).wait_recv()
            z = yown[c, s, chip]
            for k in range(1, chips):
                z = z + yrecv[c, s, chip_at(k)].astype(jnp.float32)
            for i in range(2):
                zsend[c, s, i] = z[i * steps : (i + 1) * steps].astype(zsend.dtype)

            @pl.loop(1, nt)
            def _(k):
                peer = lax.rem(t + nt + k * (1 - 2 * far), nt)
                q_copy(c, s, core, peer).start()
                q_copy(c, s, 1 - core, peer).start()

            q_copy(c, s, 1 - core, t).start()
            qbuf[c, s, mine] = zsend[c, s, core]

    drains.append(whole(ysend.at[:, :, pl.ds(0, chips - 1)], sy_s, sy_r.at[0, 0]).wait_send)
    drains.append(whole(qbuf.at[:, :, pl.ds(0, 2 * nt - 1)], sq_s, sq_r.at[0, 0]).wait_send)

    band = group * steps
    owned = heads * steps
    position = t * ctx + lax.broadcasted_iota(jnp.int32, (1, ctx), 1)
    eye = lax.broadcasted_iota(jnp.int32, (owned, HD), 0) == lax.broadcasted_iota(
        jnp.int32, (owned, HD), 1
    )

    def a_copy(peer, s):
        return pltpu.make_async_remote_copy(
            src_ref=asend.at[s, peer],
            dst_ref=arecv.at[s, t],
            send_sem=sa_s,
            recv_sem=sa_r,
            device_id=(d, peer),
            device_id_type=MESH,
        )

    def s_copy(peer, s):
        return pltpu.make_async_remote_copy(
            src_ref=ssend.at[s, peer],
            dst_ref=srecv.at[s, t],
            send_sem=ss_s,
            recv_sem=ss_r,
            device_id=(d, peer),
            device_id_type=MESH,
        )

    def attend(g, s):
        base = pl.multiple_of((g * seqs + s) * band, band)
        q = q_sc[pl.ds(base, band), :].astype(jnp.bfloat16)
        scores = lax.dot_general(
            q, kv[s, g, :, :HD], (((1,), (1,)), ((), ())), preferred_element_type=jnp.float32
        )
        masked = jnp.where(position < lengths[s], scores, NEG)
        best = jnp.max(masked, axis=-1, keepdims=True)
        weights = jnp.exp2((masked - best) * (scale * 1.4426950408889634))
        best = best * scale
        total = jnp.sum(weights, axis=-1, keepdims=True)
        acc = jnp.dot(
            weights.astype(jnp.bfloat16), kv[s, g, :, HD:], preferred_element_type=jnp.float32
        )
        for i in range(per):
            lines = slice(i * owned, (i + 1) * owned)
            asend[s, g * per + i] = acc[lines].astype(asend.dtype)
            for at, stat in enumerate((best, total)):
                ssend[s, g * per + i, at : at + 1, :] = jnp.sum(
                    jnp.where(eye, stat[lines], 0.0), axis=0, keepdims=True
                )

    side = kvh // 2 // cuts
    per = group // heads
    pltpu.make_async_copy(cache, kv, sem_kv).wait()
    for c in range(cuts):
        sides = (c, 2 * cuts - 1 - c)
        ready = [i * side + j for i in sides for j in range(side)]
        for s in range(seqs):
            whole(qbuf.at[c, s, pl.ds(0, 2 * nt - 1)], sq_s, sq_r.at[c, s]).wait_recv()
            for i in range(2):
                total = qbuf[c, s, i * nt].astype(jnp.float32)
                for j in range(1, nt):
                    total = total + qbuf[c, s, i * nt + j].astype(jnp.float32)
                for j in range(wide // HD):
                    g = sides[i] * side + j // group
                    r = ((g * seqs + s) * group + j % group) * steps
                    q_sc[r : r + steps, :] = total[:, j * HD : (j + 1) * HD]
            for low, high in zip(ready, ready[::-1]):
                attend(low + (high - low) * far, s)
                for i in range(per):
                    j = (low + (high - low) * far) * per + i

                    @pl.when(t != j)
                    def _():
                        a_copy(j, s).start()
                        s_copy(j, s).start()

    def mine_at(s):
        r = (t * heads // group * seqs + s) * band + lax.rem(t * heads, group) * steps
        return pl.ds(pl.multiple_of(r, owned), owned)

    q_own = jnp.concatenate([q_sc[mine_at(s), :] for s in range(seqs)]).astype(jnp.bfloat16)
    new_keys = fresh[:, :HD].astype(jnp.bfloat16)
    new_values = fresh[:, HD:].astype(jnp.bfloat16)
    new_scores = (
        lax.dot_general(
            q_own, new_keys, (((1,), (1,)), ((), ())), preferred_element_type=jnp.float32
        )
        * scale
    )
    row = lax.broadcasted_iota(jnp.int32, new_scores.shape, 0)
    col = lax.broadcasted_iota(jnp.int32, new_scores.shape, 1)
    col_row = col // kvh
    causal = (
        (lax.rem(col, kvh) == t * heads // group)
        & (row // owned == lax.rem(col_row, seqs))
        & (lax.rem(row, steps) >= col_row // seqs)
    )
    new_masked = jnp.where(causal, new_scores, NEG)
    top = jnp.max(new_masked, axis=-1, keepdims=True)
    new_weights = jnp.where(causal, jnp.exp(new_masked - top), 0.0)
    denom = jnp.sum(new_weights, axis=-1, keepdims=True)
    accum = jnp.dot(
        new_weights.astype(jnp.bfloat16), new_values, preferred_element_type=jnp.float32
    )

    def join(state, best, total, acc):
        top, denom, accum = state
        peak = jnp.maximum(top, best)
        left = jnp.exp(top - peak)
        right = jnp.exp(best - peak)
        return peak, denom * left + total * right, accum * left + acc * right

    def gathered(parts, stats):
        best, total = (
            jnp.concatenate(
                [
                    jnp.sum(jnp.where(eye, x[at : at + 1, :], 0.0), axis=1, keepdims=True)
                    for x in stats
                ]
            )
            for at in range(2)
        )
        return best, total, jnp.concatenate([x.astype(jnp.float32) for x in parts])

    state = join(
        (top, denom, accum),
        *gathered([asend[s, t] for s in range(seqs)], [ssend[s, t] for s in range(seqs)]),
    )
    a_all = whole(arecv.at[:, pl.ds(0, nt - 1)], sa_s, sa_r)
    s_all = whole(srecv.at[:, pl.ds(0, nt - 1)], ss_s, ss_r)
    a_all.wait_recv()
    s_all.wait_recv()

    def a_join(k, state):
        peer = lax.rem(t + k, nt)
        return join(
            state,
            *gathered([arecv[s, peer] for s in range(seqs)], [srecv[s, peer] for s in range(seqs)]),
        )

    top, denom, accum = lax.fori_loop(1, nt, a_join, state)
    r_sc[...] = accum / denom
    for j in range(heads):
        for i in range(steps):
            lines = pl.ds(j * steps + i, seqs, stride=owned)
            out[i, :, j * HD : (j + 1) * HD] = r_sc[lines, :].astype(out.dtype)

    drains.append(a_all.wait_send)
    drains.append(s_all.wait_send)
    for drain in drains:
        drain()


def body(wq_flat, hidden, cache, new_kv, lengths):
    nt = lax.axis_size("tensor")
    n = lax.axis_size("dp")
    t = lax.axis_index("tensor")
    steps, seqs, width = hidden.shape
    rows = steps * seqs
    depth, columns = wq_flat.shape
    kvh, ctx = cache.shape[1], cache.shape[2]
    half = columns // 2
    cuts = 2 if kvh % 4 == 0 else 1
    wide = half // cuts
    heads = QH // nt
    owned = heads * steps
    chips = n // 2
    bf16, f32 = jnp.bfloat16, jnp.float32
    dma = pltpu.SemaphoreType.DMA
    vmem = pl.BlockSpec(memory_space=pltpu.VMEM)
    blocked = depth % 128 != 0
    blocks = hidden
    if blocked:
        blocks = hidden.transpose(1, 0, 2).reshape(rows, n, nt, depth)
        blocks = lax.dynamic_index_in_dim(blocks, t, 2, keepdims=False).astype(f32)
        blocks = blocks.transpose(1, 0, 2)
    tiles = 1 if blocked else depth // HD
    held = (rows, depth) if blocked else (steps, seqs, depth)
    anywhere = pl.BlockSpec(memory_space=pl.ANY)
    result = pl.pallas_call(
        functools.partial(kernel, n, nt, blocked),
        out_shape=pltpu.VMEM((steps, seqs, heads * HD), f32),
        in_specs=[anywhere, anywhere, vmem if blocked else anywhere, anywhere, anywhere, anywhere],
        out_specs=vmem,
        scratch_shapes=[
            pltpu.VMEM(hidden.shape, bf16),
            pltpu.VMEM(new_kv.shape, bf16),
            pltpu.SMEM(lengths.shape, jnp.int32),
            dma((3,)),
            pltpu.VMEM((depth, half), bf16),
            pltpu.VMEM((2, depth, half), bf16),
            pltpu.VMEM(cache.shape, bf16),
            pltpu.VMEM((rows * kvh, 2 * HD), f32),
            pltpu.VMEM((2, tiles, n * rows, depth // tiles), f32),
            pltpu.VMEM((2, n, *held), blocks.dtype),
            pltpu.VMEM((cuts, seqs, chips, 2 * steps, wide), f32),
            pltpu.VMEM((cuts, seqs, chips, 2 * steps, wide), bf16),
            pltpu.VMEM((cuts, seqs, chips, 2 * steps, wide), bf16),
            pltpu.VMEM((cuts, seqs, 2, steps, wide), bf16),
            pltpu.VMEM((cuts, seqs, 2 * nt, steps, wide), bf16),
            pltpu.VMEM((QH * rows, HD), f32),
            pltpu.VMEM((heads * rows, HD), f32),
            pltpu.VMEM((seqs, nt, owned, HD), bf16),
            pltpu.VMEM((seqs, nt, owned, HD), bf16),
            pltpu.VMEM((seqs, nt, 8, HD), f32),
            pltpu.VMEM((seqs, nt, 8, HD), f32),
            dma((2,)),
            dma(()),
            dma(()),
            dma(()),
            dma(()),
            dma((cuts, seqs)),
            dma(()),
            dma(()),
            dma(()),
            dma((cuts, seqs)),
            dma(()),
            dma(()),
            dma(()),
            dma(()),
        ],
        compiler_params=pltpu.CompilerParams(collective_id=0, has_side_effects=True),
    )(lengths, hidden, blocks, new_kv, wq_flat, cache)
    return result.astype(bf16)


def solution(mesh):
    placed = (
        P(("dp", "tensor"), None),
        P(None, "dp", None),
        P("dp", None, "tensor", None),
        P(None, "dp", None, None),
        P("dp"),
    )
    return jax.shard_map(
        body, mesh=mesh, in_specs=placed, out_specs=P(None, "dp", "tensor"), check_vma=False
    )
```

```python
import functools

import jax
import jax.numpy as jnp
from jax import lax
from jax.experimental import pallas as pl
from jax.experimental.pallas import tpu as pltpu
from jax.sharding import PartitionSpec as P

QH = 32
HD = 128
MESH = pl.DeviceIdType.MESH
NEG = -1e30


def kernel(
    n,
    nt,
    blocked,
    lengths_any,
    hid_any,
    blocks,
    new_any,
    wq,
    cache,
    out,
    hid,
    new_kv,
    lengths,
    sem_in,
    wq_out,
    wq_all,
    kv,
    fresh,
    x_sc,
    xg,
    yown,
    ysend,
    yrecv,
    zsend,
    qbuf,
    q_sc,
    r_sc,
    asend,
    arecv,
    ssend,
    srecv,
    sem_w,
    sem_kv,
    sx_s,
    sx_r,
    sy_s,
    sy_r,
    sp_s,
    sp_r,
    sq_s,
    sq_r,
    sa_s,
    sa_r,
    ss_s,
    ss_r,
):
    d = lax.axis_index("dp")
    t = lax.axis_index("tensor")
    core = lax.rem(d, 2)
    chip = d // 2
    chips = n // 2
    mate = d + 1 - 2 * core
    steps, seqs, width = hid.shape
    _, depth, half = wq_all.shape
    rows = steps * seqs
    _, kvh, ctx, _ = kv.shape
    drains = []
    heads = QH // nt
    group = QH // kvh
    scale = 1.0 / HD**0.5

    load_hid = pltpu.make_async_copy(hid_any, hid, sem_in.at[0])
    load_new = pltpu.make_async_copy(new_any, new_kv, sem_in.at[1])
    load_lengths = pltpu.make_async_copy(lengths_any, lengths, sem_in.at[2])
    load_hid.start()
    load_lengths.start()
    load_new.start()
    load_out = pltpu.make_async_copy(
        wq.at[:, pl.ds(pl.multiple_of((1 - core) * half, half), half)], wq_out, sem_w.at[0]
    )
    load_own = pltpu.make_async_copy(
        wq.at[:, pl.ds(pl.multiple_of(core * half, half), half)], wq_all.at[core], sem_w.at[1]
    )
    load_out.start()
    load_own.start()
    load_kv = [
        [pltpu.make_async_copy(cache.at[s, g], kv.at[s, g], sem_kv) for g in range(kvh)]
        for s in range(seqs)
    ]
    barrier = pltpu.get_barrier_semaphore()

    @pl.loop(1, n)
    def _(k):
        pl.semaphore_signal(
            barrier, inc=1, device_id=(lax.rem(d + k, n), t), device_id_type=MESH
        )

    @pl.loop(1, nt)
    def _(k):
        peer = lax.rem(t + k, nt)
        pl.semaphore_signal(barrier, inc=1, device_id=(d, peer), device_id_type=MESH)
        pl.semaphore_signal(barrier, inc=1, device_id=(mate, peer), device_id_type=MESH)

    pl.semaphore_wait(barrier, n - 1 + 2 * (nt - 1))

    load_hid.wait()
    load_new.wait()
    load_lengths.wait()

    def columns_of(block):
        if blocked:
            return blocks.at[block]
        start = pl.multiple_of((block * nt + t) * depth, depth)
        return hid.at[:, :, pl.ds(start, depth)]

    def whole(ref, send_sem, recv_sem):
        return pltpu.make_async_remote_copy(
            src_ref=ref,
            dst_ref=ref,
            send_sem=send_sem,
            recv_sem=recv_sem,
            device_id=(mate, t),
            device_id_type=MESH,
        )

    def chip_at(k):
        return lax.rem(chip % 2 + k % 2, 2) + 2 * lax.rem(chip // 2 + k // 2, chips // 2)

    def peer_at(k):
        return 2 * chip_at(k // 2) + lax.rem(core + k % 2, 2)

    def x_copy(b, peer):
        return pltpu.make_async_remote_copy(
            src_ref=columns_of(2 * (peer // 2) + b),
            dst_ref=xg.at[b, d],
            send_sem=sx_s,
            recv_sem=sx_r,
            device_id=(peer, t),
            device_id_type=MESH,
        )

    push = pltpu.make_async_remote_copy(
        src_ref=wq_out,
        dst_ref=wq_all.at[core],
        send_sem=sp_s,
        recv_sem=sp_r,
        device_id=(mate, t),
        device_id_type=MESH,
    )
    @pl.loop(1, n)
    def _(k):
        for b in range(2):
            x_copy(b, peer_at(n - k)).start()

    load_out.wait()
    push.start()
    for b in range(2):
        xg[b, d] = columns_of(2 * chip + b)[...]
    for i in range(steps):
        for s in range(seqs):
            r = (i * seqs + s) * kvh
            fresh[r : r + kvh, :] = new_kv[i, s].astype(jnp.float32)
    load_own.wait()
    push.wait_recv()

    x_all = whole(xg.at[:, pl.ds(0, n - 1)], sx_s, sx_r)
    x_all.wait_recv()
    drains.append(push.wait_send)
    drains.append(x_all.wait_send)
    _, tiles, _, lanes = x_sc.shape
    xs = []
    for b in range(2):
        for p in range(n):
            if blocked:
                for s in range(seqs):
                    r = (s * n + p) * steps
                    x_sc[b, 0, r : r + steps, :] = xg[b, p, s * steps : (s + 1) * steps]
            else:
                for i in range(steps):
                    lines = pl.ds(p * steps + i, seqs, stride=n * steps)
                    block = xg[b, p, i].astype(jnp.float32)
                    for h in range(tiles):
                        x_sc.at[b, h][lines, :] = block[:, h * lanes : (h + 1) * lanes]
        xs.append(jnp.concatenate([x_sc[b, h] for h in range(tiles)], axis=1).astype(jnp.bfloat16))

    cuts = ysend.shape[0]
    wide = half // cuts

    def y_copy(c, s, peer):
        return pltpu.make_async_remote_copy(
            src_ref=ysend.at[c, s, peer],
            dst_ref=yrecv.at[c, s, chip],
            send_sem=sy_s,
            recv_sem=sy_r.at[c, s],
            device_id=(2 * peer + core, t),
            device_id_type=MESH,
        )

    for c in range(cuts):
        at = c + core * (cuts - 1 - 2 * c)
        columns = pl.ds(pl.multiple_of(at * wide, wide), wide)
        y = sum(
            jnp.dot(xs[b], wq_all[b, :, columns], preferred_element_type=jnp.float32)
            for b in range(2)
        ).reshape(seqs, chips, 2 * steps, wide)
        for s in range(seqs):
            ysend[c, s] = y[s].astype(jnp.bfloat16)
            yown[c, s] = y[s]

            for k in range(1, chips):
                y_copy(c, s, chip_at(chips - k)).start()

    for g in range(kvh):
        for s in range(seqs):
            load_kv[s][g].start()
    mine = core * nt + t
    far = (2 * t < nt).astype(jnp.int32)

    def q_copy(c, s, peer_core, peer):
        return pltpu.make_async_remote_copy(
            src_ref=zsend.at[c, s, peer_core],
            dst_ref=qbuf.at[c, s, mine],
            send_sem=sq_s,
            recv_sem=sq_r.at[c, s],
            device_id=(2 * chip + peer_core, peer),
            device_id_type=MESH,
        )

    for c in range(cuts):
        for s in range(seqs):
            whole(yrecv.at[c, s, pl.ds(0, chips - 1)], sy_s, sy_r.at[c, s]).wait_recv()
            z = yown[c, s, chip]
            for k in range(1, chips):
                z = z + yrecv[c, s, chip_at(k)].astype(jnp.float32)
            for i in range(2):
                zsend[c, s, i] = z[i * steps : (i + 1) * steps].astype(zsend.dtype)

            for k in range(1, nt):
                peer = lax.rem(t + nt + k * (1 - 2 * far), nt)
                q_copy(c, s, core, peer).start()
                q_copy(c, s, 1 - core, peer).start()

            q_copy(c, s, 1 - core, t).start()
            qbuf[c, s, mine] = zsend[c, s, core]

    drains.append(whole(ysend.at[:, :, pl.ds(0, chips - 1)], sy_s, sy_r.at[0, 0]).wait_send)
    drains.append(whole(qbuf.at[:, :, pl.ds(0, 2 * nt - 1)], sq_s, sq_r.at[0, 0]).wait_send)

    band = group * steps
    owned = heads * steps
    position = t * ctx + lax.broadcasted_iota(jnp.int32, (1, ctx), 1)
    eye = lax.broadcasted_iota(jnp.int32, (owned, HD), 0) == lax.broadcasted_iota(
        jnp.int32, (owned, HD), 1
    )

    def a_copy(peer, s):
        return pltpu.make_async_remote_copy(
            src_ref=asend.at[s, peer],
            dst_ref=arecv.at[s, t],
            send_sem=sa_s,
            recv_sem=sa_r,
            device_id=(d, peer),
            device_id_type=MESH,
        )

    def s_copy(peer, s):
        return pltpu.make_async_remote_copy(
            src_ref=ssend.at[s, peer],
            dst_ref=srecv.at[s, t],
            send_sem=ss_s,
            recv_sem=ss_r,
            device_id=(d, peer),
            device_id_type=MESH,
        )

    def attend(g, s):
        base = pl.multiple_of((g * seqs + s) * band, band)
        q = q_sc[pl.ds(base, band), :].astype(jnp.bfloat16)
        scores = lax.dot_general(
            q, kv[s, g, :, :HD], (((1,), (1,)), ((), ())), preferred_element_type=jnp.float32
        )
        masked = jnp.where(position < lengths[s], scores, NEG)
        best = jnp.max(masked, axis=-1, keepdims=True)
        weights = jnp.exp2((masked - best) * (scale * 1.4426950408889634))
        best = best * scale
        total = jnp.sum(weights, axis=-1, keepdims=True)
        acc = jnp.dot(
            weights.astype(jnp.bfloat16), kv[s, g, :, HD:], preferred_element_type=jnp.float32
        )
        for i in range(per):
            lines = slice(i * owned, (i + 1) * owned)
            asend[s, g * per + i] = acc[lines].astype(asend.dtype)
            for at, stat in enumerate((best, total)):
                ssend[s, g * per + i, at : at + 1, :] = jnp.sum(
                    jnp.where(eye, stat[lines], 0.0), axis=0, keepdims=True
                )

    side = kvh // 2 // cuts
    per = group // heads
    pltpu.make_async_copy(cache, kv, sem_kv).wait()
    for c in range(cuts):
        sides = (c, 2 * cuts - 1 - c)
        ready = [i * side + j for i in sides for j in range(side)]
        for s in range(seqs):
            whole(qbuf.at[c, s, pl.ds(0, 2 * nt - 1)], sq_s, sq_r.at[c, s]).wait_recv()
            for i in range(2):
                total = qbuf[c, s, i * nt].astype(jnp.float32)
                for j in range(1, nt):
                    total = total + qbuf[c, s, i * nt + j].astype(jnp.float32)
                for j in range(wide // HD):
                    g = sides[i] * side + j // group
                    r = ((g * seqs + s) * group + j % group) * steps
                    q_sc[r : r + steps, :] = total[:, j * HD : (j + 1) * HD]
            for low, high in zip(ready, ready[::-1]):
                attend(low + (high - low) * far, s)
                for i in range(per):
                    j = (low + (high - low) * far) * per + i

                    @pl.when(t != j)
                    def _():
                        a_copy(j, s).start()
                        s_copy(j, s).start()

    def mine_at(s):
        r = (t * heads // group * seqs + s) * band + lax.rem(t * heads, group) * steps
        return pl.ds(pl.multiple_of(r, owned), owned)

    q_own = jnp.concatenate([q_sc[mine_at(s), :] for s in range(seqs)]).astype(jnp.bfloat16)
    new_keys = fresh[:, :HD].astype(jnp.bfloat16)
    new_values = fresh[:, HD:].astype(jnp.bfloat16)
    new_scores = (
        lax.dot_general(
            q_own, new_keys, (((1,), (1,)), ((), ())), preferred_element_type=jnp.float32
        )
        * scale
    )
    row = lax.broadcasted_iota(jnp.int32, new_scores.shape, 0)
    col = lax.broadcasted_iota(jnp.int32, new_scores.shape, 1)
    col_row = col // kvh
    causal = (
        (lax.rem(col, kvh) == t * heads // group)
        & (row // owned == lax.rem(col_row, seqs))
        & (lax.rem(row, steps) >= col_row // seqs)
    )
    new_masked = jnp.where(causal, new_scores, NEG)
    top = jnp.max(new_masked, axis=-1, keepdims=True)
    new_weights = jnp.where(causal, jnp.exp(new_masked - top), 0.0)
    denom = jnp.sum(new_weights, axis=-1, keepdims=True)
    accum = jnp.dot(
        new_weights.astype(jnp.bfloat16), new_values, preferred_element_type=jnp.float32
    )

    def join(state, best, total, acc):
        top, denom, accum = state
        peak = jnp.maximum(top, best)
        left = jnp.exp(top - peak)
        right = jnp.exp(best - peak)
        return peak, denom * left + total * right, accum * left + acc * right

    def gathered(parts, stats):
        best, total = (
            jnp.concatenate(
                [
                    jnp.sum(jnp.where(eye, x[at : at + 1, :], 0.0), axis=1, keepdims=True)
                    for x in stats
                ]
            )
            for at in range(2)
        )
        return best, total, jnp.concatenate([x.astype(jnp.float32) for x in parts])

    state = join(
        (top, denom, accum),
        *gathered([asend[s, t] for s in range(seqs)], [ssend[s, t] for s in range(seqs)]),
    )
    a_all = whole(arecv.at[:, pl.ds(0, nt - 1)], sa_s, sa_r)
    s_all = whole(srecv.at[:, pl.ds(0, nt - 1)], ss_s, ss_r)
    a_all.wait_recv()
    s_all.wait_recv()

    def a_join(k, state):
        peer = lax.rem(t + k, nt)
        return join(
            state,
            *gathered([arecv[s, peer] for s in range(seqs)], [srecv[s, peer] for s in range(seqs)]),
        )

    for k in range(1, nt):
        state = a_join(k, state)
    top, denom, accum = state
    r_sc[...] = accum / denom
    for j in range(heads):
        for i in range(steps):
            lines = pl.ds(j * steps + i, seqs, stride=owned)
            out[i, :, j * HD : (j + 1) * HD] = r_sc[lines, :].astype(out.dtype)

    drains.append(a_all.wait_send)
    drains.append(s_all.wait_send)
    for drain in drains:
        drain()


def body(wq_flat, hidden, cache, new_kv, lengths):
    nt = lax.axis_size("tensor")
    n = lax.axis_size("dp")
    t = lax.axis_index("tensor")
    steps, seqs, width = hidden.shape
    rows = steps * seqs
    depth, columns = wq_flat.shape
    kvh, ctx = cache.shape[1], cache.shape[2]
    half = columns // 2
    cuts = 2 if kvh % 4 == 0 else 1
    wide = half // cuts
    heads = QH // nt
    owned = heads * steps
    chips = n // 2
    bf16, f32 = jnp.bfloat16, jnp.float32
    dma = pltpu.SemaphoreType.DMA
    vmem = pl.BlockSpec(memory_space=pltpu.VMEM)
    blocked = depth % 128 != 0
    blocks = hidden
    if blocked:
        blocks = hidden.transpose(1, 0, 2).reshape(rows, n, nt, depth)
        blocks = lax.dynamic_index_in_dim(blocks, t, 2, keepdims=False).astype(f32)
        blocks = blocks.transpose(1, 0, 2)
    tiles = 1 if blocked else depth // HD
    held = (rows, depth) if blocked else (steps, seqs, depth)
    anywhere = pl.BlockSpec(memory_space=pl.ANY)
    result = pl.pallas_call(
        functools.partial(kernel, n, nt, blocked),
        out_shape=pltpu.VMEM((steps, seqs, heads * HD), f32),
        in_specs=[anywhere, anywhere, vmem if blocked else anywhere, anywhere, anywhere, anywhere],
        out_specs=vmem,
        scratch_shapes=[
            pltpu.VMEM(hidden.shape, bf16),
            pltpu.VMEM(new_kv.shape, bf16),
            pltpu.SMEM(lengths.shape, jnp.int32),
            dma((3,)),
            pltpu.VMEM((depth, half), bf16),
            pltpu.VMEM((2, depth, half), bf16),
            pltpu.VMEM(cache.shape, bf16),
            pltpu.VMEM((rows * kvh, 2 * HD), f32),
            pltpu.VMEM((2, tiles, n * rows, depth // tiles), f32),
            pltpu.VMEM((2, n, *held), blocks.dtype),
            pltpu.VMEM((cuts, seqs, chips, 2 * steps, wide), f32),
            pltpu.VMEM((cuts, seqs, chips, 2 * steps, wide), bf16),
            pltpu.VMEM((cuts, seqs, chips, 2 * steps, wide), bf16),
            pltpu.VMEM((cuts, seqs, 2, steps, wide), bf16),
            pltpu.VMEM((cuts, seqs, 2 * nt, steps, wide), bf16),
            pltpu.VMEM((QH * rows, HD), f32),
            pltpu.VMEM((heads * rows, HD), f32),
            pltpu.VMEM((seqs, nt, owned, HD), bf16),
            pltpu.VMEM((seqs, nt, owned, HD), bf16),
            pltpu.VMEM((seqs, nt, 8, HD), f32),
            pltpu.VMEM((seqs, nt, 8, HD), f32),
            dma((2,)),
            dma(()),
            dma(()),
            dma(()),
            dma(()),
            dma((cuts, seqs)),
            dma(()),
            dma(()),
            dma(()),
            dma((cuts, seqs)),
            dma(()),
            dma(()),
            dma(()),
            dma(()),
        ],
        compiler_params=pltpu.CompilerParams(collective_id=0, has_side_effects=True),
    )(lengths, hidden, blocks, new_kv, wq_flat, cache)
    return result.astype(bf16)


def solution(mesh):
    placed = (
        P(("dp", "tensor"), None),
        P(None, "dp", None),
        P("dp", None, "tensor", None),
        P(None, "dp", None, None),
        P("dp"),
    )
    return jax.shard_map(
        body, mesh=mesh, in_specs=placed, out_specs=P(None, "dp", "tensor"), check_vma=False
    )
```
